32 devices in a mesh: pix: 16 (over z, y, core), tm: 2 (over x).
Axes of the slice: x: 2, y: 2, z: 4, core: 2. Of those that a mesh axis runs over, the one named last changes fastest.
Arguments:
- iq: bfloat16 [600, 2, 65536], P('tm', None, 'pix'), as said below
- tail_frames: bfloat16 [150, 2, 65536], P(None, None, 'pix'), as said below
- start_basis: float32 [300, 128], replicated, may hold values from -6 to 6
- low_rank: int32 [4], P('tm'), may hold values from 1 to 32
- high_rank: int32 [4], P('tm'), may hold values from 64 to 128
Outputs:
- power: float32 [4, 65536], P('tm', 'pix')
- basis: float32 [4, 300, 128], P('tm')
The draws below stay inside these ranges and needn't reach their ends.
Inputs may be any that keep to these rules, and one draw needn't show every extreme that they name: low_rank[w] < high_rank[w] <= 128 for every window. `iq`: real-valued samples of order one. `tail_frames`: real-valued samples of order one, continuing iq.
All inputs are finite; a program needn't handle non-finite values.
Results may differ from the reference program's by a relative error of at most 0.0008.
Values may be sent and summed in bfloat16 or wider, within the bound.
A program may use at most 128 MiB of HBM per device.

```python
import math
import jax
import jax.numpy as jnp
from jax import lax

W = 300
HOP = 150
K = 128
ITERS = 3
PIX_DEV = 4096
NPIX = 65536
NWIN = 4
FRAMES = 600


def acquisition(key):
    base = jax.random.fold_in(key, 11)
    keys = jax.random.split(base, 6)
    total = FRAMES + HOP
    noise = jax.random.normal(keys[0], (total, 2, NPIX), jnp.float32)
    scale = jnp.exp(jax.random.uniform(keys[1], (NPIX,), jnp.float32, math.log(0.5), math.log(3.0)))
    blocks = NPIX // PIX_DEV
    gain = jnp.exp(jax.random.uniform(keys[2], (total, blocks), jnp.float32, math.log(0.5), math.log(2.0)))
    gain = jnp.repeat(gain, PIX_DEV, axis=1)
    omega = jax.random.uniform(keys[3], (4,), jnp.float32, 0.002, 0.03)
    amplitude = 0.3 * jax.random.normal(keys[4], (4, NPIX), jnp.float32)
    phase = jax.random.uniform(keys[5], (4, NPIX), jnp.float32, -math.pi, math.pi)
    frame = jnp.arange(total, dtype=jnp.float32)[:, None]
    real_part = jnp.zeros((total, NPIX), jnp.float32)
    imag_part = jnp.zeros((total, NPIX), jnp.float32)
    for index in range(4):
        angle = omega[index] * frame + phase[index][None, :]
        real_part = real_part + amplitude[index][None, :] * jnp.cos(angle)
        imag_part = imag_part + amplitude[index][None, :] * jnp.sin(angle)
    clutter = jnp.stack([real_part, imag_part], axis=1)
    return (noise * gain[:, None, :] + clutter) * scale[None, None, :]


def draw_iq(key, part):
    return acquisition(key)[:FRAMES].astype(jnp.bfloat16)


def draw_tail_frames(key, part):
    return acquisition(key)[FRAMES:].astype(jnp.bfloat16)


def place_ends(result, rng, smallest, top_value):
    place = [jax.random.randint(jax.random.fold_in(rng, axis), (), 0, length) for axis, length in enumerate(result.shape)]
    longest = result.shape.index(max(result.shape))
    neighbour = place[:longest] + [(place[longest] + 1) % result.shape[longest]] + place[longest + 1:]
    return result.at[tuple(place)].set(smallest).at[tuple(neighbour)].set(top_value)


def normal_values(own_key, shape, deviation, limit, held_as=jnp.bfloat16):
    values = jax.random.normal(own_key, shape, jnp.float32) * deviation
    return jnp.minimum(jnp.maximum(values, -limit), limit).astype(held_as)


def setup_inputs(seed: int = 0) -> dict:
    streams_of = jax.random.split(jax.random.key(seed), 6)
    return {
        "iq": draw_iq(jax.random.fold_in(streams_of[5], 71), 0),
        "tail_frames": draw_tail_frames(jax.random.fold_in(streams_of[5], 71), 0),
        "start_basis": normal_values(streams_of[2], (W, K), 1.0, 6.0, jnp.float32),
        "low_rank": place_ends(jax.random.randint(streams_of[3], (NWIN,), 1, K // 4 + 1), jax.random.fold_in(streams_of[3], 1), 1, (K // 4 + 1) - 1).astype(jnp.int32),
        "high_rank": place_ends(jax.random.randint(streams_of[4], (NWIN,), K // 2, K + 1), jax.random.fold_in(streams_of[4], 1), K // 2, K).astype(jnp.int32),
    }


def iterate(gram, start):
    basis = start
    for step in range(ITERS):
        image = jnp.dot(gram, basis, precision=lax.Precision.HIGHEST)
        inner = jnp.dot(image.T, image, precision=lax.Precision.HIGHEST)
        factor = jnp.linalg.cholesky(inner)
        basis = lax.linalg.triangular_solve(factor, image, left_side=False, lower=True, transpose_a=True)
    return basis

def reference(iq, tail_frames, start_basis, low_rank, high_rank):
    extended = jnp.concatenate([iq, tail_frames], axis=0)
    columns = jnp.arange(K, dtype=jnp.int32)
    powers = []
    bases = []
    for window in range(NWIN):
        casorati = extended[window * HOP:window * HOP + W].reshape(W, 2 * NPIX)
        gram = jnp.dot(casorati.astype(jnp.float32), casorati.T.astype(jnp.float32), preferred_element_type=jnp.float32)
        basis = iterate(gram, start_basis)
        keep = ((columns >= low_rank[window]) & (columns < high_rank[window])).astype(jnp.float32)
        proj = jnp.dot(basis * keep[None, :], basis.T, precision=lax.Precision.HIGHEST).astype(jnp.bfloat16)
        filtered = jnp.dot(proj.astype(jnp.float32), casorati.astype(jnp.float32), preferred_element_type=jnp.float32)
        powers.append(jnp.sum((filtered * filtered).reshape(W, 2, NPIX), axis=(0, 1)) / W)
        bases.append(basis)
    return (jnp.stack(powers), jnp.stack(bases))
```

```python
import functools

import jax
import jax.numpy as jnp
from jax import lax
from jax.experimental import pallas as pl
from jax.experimental.pallas import tpu as pltpu
from jax.sharding import PartitionSpec as P

K = 128
ITERS = 3
WIN_DEV = 2
SUB = 8
HI = lax.Precision.HIGHEST


def from_behind(block, axis, distance):
    devices = range(lax.axis_size(axis))
    route = [(i - distance, i) for i in devices if i - distance in devices]
    return lax.ppermute(block, axis, route)


def dot(a, b, ca, cb):
    return lax.dot_general(
        a, b, (((ca,), (cb,)), ((), ())), precision=HI, preferred_element_type=jnp.float32
    )


def inverse_factors(grams):
    tiles = K // SUB
    lane = lax.broadcasted_iota(jnp.int32, (SUB, K), 1)
    sub = lax.broadcasted_iota(jnp.int32, (SUB, K), 0)
    work = [[m[SUB * u : SUB * u + SUB, :] for u in range(tiles)] for m in grams]
    for j in range(K):
        t, s = divmod(j, SUB)
        here = lane == j
        for rows in work:
            pivot = rows[t][s : s + 1, j : j + 1]
            scaled = jnp.where(here[:1], 1.0, rows[t][s : s + 1, :]) * (1.0 / pivot)
            for u in range(t, tiles):
                if u == t and s == SUB - 1:
                    continue
                column = rows[u][:, j : j + 1]
                update = jnp.where(here, 0.0, rows[u]) - column * scaled
                rows[u] = jnp.where(sub > s, update, rows[u]) if u == t else update
    inverses = []
    for rows in work:
        out = []
        for u in range(tiles):
            row = sub + SUB * u
            diagonal = jnp.sum(jnp.where(lane == row, rows[u], 0.0), axis=1, keepdims=True)
            unit = jnp.where(lane < row, rows[u], jnp.where(lane == row, 1.0, 0.0))
            out.append(unit * lax.rsqrt(diagonal))
        inverses.append(jnp.concatenate(out, axis=0))
    return inverses


def iterate_kernel(low_ref, high_ref, gram_ref, start_ref, basis_ref, proj_ref):
    windows = range(WIN_DEV)
    for window in windows:
        basis_ref[window] = start_ref[...]

    def step(_, carry):
        images = [dot(gram_ref[w], basis_ref[w], 1, 0) for w in windows]
        inverses = inverse_factors([dot(z, z, 0, 0) for z in images])
        for w in windows:
            basis_ref[w] = dot(images[w], inverses[w], 1, 1)
        return carry

    lax.fori_loop(0, ITERS, step, 0)
    columns = lax.broadcasted_iota(jnp.int32, (1, K), 1)
    for w in windows:
        basis = basis_ref[w]
        keep = ((columns >= low_ref[w]) & (columns < high_ref[w])).astype(jnp.float32)
        proj_ref[w] = dot(basis * keep, basis, 1, 1).astype(jnp.bfloat16)


def iterate(grams, start, low, high):
    width = start.shape[0]
    smem = pl.BlockSpec(memory_space=pltpu.SMEM)
    vmem = pl.BlockSpec(memory_space=pltpu.VMEM)
    return pl.pallas_call(
        iterate_kernel,
        out_shape=(
            jax.ShapeDtypeStruct((WIN_DEV, width, K), jnp.float32),
            jax.ShapeDtypeStruct((WIN_DEV, width, width), jnp.bfloat16),
        ),
        in_specs=[smem, smem, vmem, vmem],
        out_specs=(vmem, vmem),
        name="iterate",
    )(low, high, grams, start)


def body(iq, tail_frames, start_basis, low_rank, high_rank):
    half = iq.shape[0] // WIN_DEV
    width = 2 * half
    incoming = from_behind(iq[:half], "tm", -1)
    at_end = lax.axis_index("tm") == lax.axis_size("tm") - 1
    following = jnp.where(at_end, tail_frames, incoming)
    extended = jnp.concatenate([iq, following], axis=0)
    casoratis = [
        extended[window * half : window * half + width].reshape(width, -1)
        for window in range(WIN_DEV)
    ]
    grams = []
    for matrix in casoratis:
        summed = lax.psum(
            lax.dot_general(
                matrix, matrix, (((1,), (1,)), ((), ())), preferred_element_type=jnp.float32
            ),
            "pix",
        )
        grams.append(summed)
    bases, projs = iterate(jnp.stack(grams), start_basis, low_rank, high_rank)
    powers = []
    for window in range(WIN_DEV):
        filtered = jnp.dot(projs[window], casoratis[window], preferred_element_type=jnp.float32)
        powers.append(jnp.sum((filtered * filtered).reshape(width, 2, -1), axis=(0, 1)) / width)
    return (jnp.stack(powers), bases)


def solution(mesh):
    placed = (P("tm", None, "pix"), P(None, None, "pix"), P(), P("tm"), P("tm"))
    return jax.shard_map(
        body,
        mesh=mesh,
        in_specs=placed,
        out_specs=(P("tm", "pix"), P("tm", None, None)),
        check_vma=False,
    )
```

```python
import functools

import jax
import jax.numpy as jnp
from jax import lax
from jax.experimental import pallas as pl
from jax.experimental.pallas import tpu as pltpu
from jax.sharding import PartitionSpec as P

K = 128
ITERS = 3
WIN_DEV = 2
SUB = 8
LANES = 128
BLOCKS = 5
HI = lax.Precision.HIGHEST
MESH = pl.DeviceIdType.MESH
VMEM = pl.BlockSpec(memory_space=pltpu.VMEM)
SMEM = pl.BlockSpec(memory_space=pltpu.SMEM)


def from_behind(block, axis, distance):
    devices = range(lax.axis_size(axis))
    route = [(i - distance, i) for i in devices if i - distance in devices]
    return lax.ppermute(block, axis, route)


def dot(a, b, ca, cb, precision=HI):
    return lax.dot_general(
        a, b, (((ca,), (cb,)), ((), ())), precision=precision, preferred_element_type=jnp.float32
    )


def up(value, unit):
    return -(-value // unit) * unit


def gram_kernel(half, own_ref, next_ref, packed_ref, acc):
    step = pl.program_id(0)

    @pl.when(step == 0)
    def _():
        acc[...] = jnp.zeros_like(acc)

    first, second, third = own_ref[0], own_ref[1], next_ref[...]
    pairs = ((first, first), (first, second), (second, second), (second, third), (third, third))
    for k, (a, b) in enumerate(pairs):
        acc[k] += dot(a, b, 1, 1, None)

    @pl.when(step == pl.num_programs(0) - 1)
    def _():
        pitch = up(half, SUB)
        packed_ref[...] = jnp.zeros_like(packed_ref)
        for k in range(BLOCKS):
            packed_ref[pitch * k : pitch * k + half] = acc[k, :, :LANES]
        rest = [acc[k, :, LANES:] for k in range(BLOCKS)]
        rest.append(jnp.zeros((half, LANES - BLOCKS * (half - LANES)), jnp.float32))
        packed_ref[pitch * BLOCKS : pitch * BLOCKS + half] = jnp.concatenate(rest, axis=1)


def gram_blocks(own, following, rows):
    _, half, columns = own.shape
    tile = 1024
    return pl.pallas_call(
        functools.partial(gram_kernel, half),
        out_shape=jax.ShapeDtypeStruct((rows, LANES), jnp.float32),
        grid=(columns // tile,),
        in_specs=[
            pl.BlockSpec((2, half, tile), lambda i: (0, 0, i)),
            pl.BlockSpec((half, tile), lambda i: (0, i)),
        ],
        out_specs=pl.BlockSpec((rows, LANES), lambda i: (0, 0)),
        scratch_shapes=[pltpu.VMEM((BLOCKS, half, half), jnp.float32)],
        name="gram",
    )(own, following)


def sum_kernel(n, x_ref, out_ref, acc, landed, gathered, send_sem, recv_sem):
    me = lax.axis_index("pix")
    bits = n.bit_length() - 1
    bit = [lax.rem(me // (1 << b), 2) for b in range(bits)]
    partner = [me + (1 - 2 * bit[b]) * (1 << b) for b in range(bits)]

    barrier = pltpu.get_barrier_semaphore()
    for b in range(bits):
        pl.semaphore_signal(
            barrier, inc=1, device_id={"pix": partner[b]}, device_id_type=MESH
        )
    pl.semaphore_wait(barrier, bits)

    def window(start, size):
        return pl.ds(pl.multiple_of(start, SUB), size)

    start, size, base = 0, x_ref.shape[0], 0
    for b in range(bits):
        size //= 2
        keep = start + bit[b] * size
        give = start + (1 - bit[b]) * size
        source = x_ref if b == 0 else acc
        copy = pltpu.make_async_remote_copy(
            src_ref=source.at[window(give, size)],
            dst_ref=landed.at[pl.ds(base, size)],
            send_sem=send_sem.at[b],
            recv_sem=recv_sem.at[b],
            device_id={"pix": partner[b]},
            device_id_type=MESH,
        )
        copy.start()
        copy.wait()
        target = gathered if b == bits - 1 else acc
        target[window(keep, size)] = source[window(keep, size)] + landed[pl.ds(base, size)]
        start, base = keep, base + size
    for b in reversed(range(bits)):
        copy = pltpu.make_async_remote_copy(
            src_ref=gathered.at[window(start, size)],
            dst_ref=gathered.at[window(start, size)],
            send_sem=send_sem.at[bits + b],
            recv_sem=recv_sem.at[bits + b],
            device_id={"pix": partner[b]},
            device_id_type=MESH,
        )
        copy.start()
        copy.wait()
        start, size = start - bit[b] * size, 2 * size
    out_ref[...] = gathered[...]


def sum_over_pix(packed):
    n = lax.axis_size("pix")
    bits = n.bit_length() - 1
    return pl.pallas_call(
        functools.partial(sum_kernel, n),
        out_shape=jax.ShapeDtypeStruct(packed.shape, jnp.float32),
        in_specs=[VMEM],
        out_specs=VMEM,
        scratch_shapes=[
            pltpu.VMEM(packed.shape, jnp.float32),
            pltpu.VMEM(packed.shape, jnp.float32),
            pltpu.VMEM(packed.shape, jnp.float32),
            pltpu.SemaphoreType.DMA((2 * bits,)),
            pltpu.SemaphoreType.DMA((2 * bits,)),
        ],
        compiler_params=pltpu.CompilerParams(collective_id=0, has_side_effects=True),
        name="sum_over_pix",
    )(packed)


def inverse_factors(grams):
    tiles = K // SUB
    lane = lax.broadcasted_iota(jnp.int32, (SUB, K), 1)
    sub = lax.broadcasted_iota(jnp.int32, (SUB, K), 0)
    work = [[m[SUB * u : SUB * u + SUB, :] for u in range(tiles)] for m in grams]
    for j in range(K):
        t, s = divmod(j, SUB)
        here = lane == j
        for rows in work:
            pivot = rows[t][s : s + 1, j : j + 1]
            scaled = jnp.where(here[:1], 1.0, rows[t][s : s + 1, :]) * (1.0 / pivot)
            for u in range(t, tiles):
                if u == t and s == SUB - 1:
                    continue
                column = rows[u][:, j : j + 1]
                update = jnp.where(here, 0.0, rows[u]) - column * scaled
                rows[u] = jnp.where(sub > s, update, rows[u]) if u == t else update
    inverses = []
    for rows in work:
        out = []
        for u in range(tiles):
            row = sub + SUB * u
            diagonal = jnp.sum(jnp.where(lane == row, rows[u], 0.0), axis=1, keepdims=True)
            unit = jnp.where(lane < row, rows[u], jnp.where(lane == row, 1.0, 0.0))
            out.append(unit * lax.rsqrt(diagonal))
        inverses.append(jnp.concatenate(out, axis=0))
    return inverses


def iterate_kernel(half, low_ref, high_ref, packed_ref, start_ref, basis_ref, proj_ref, gram, held):
    windows = range(WIN_DEV)
    pitch = up(half, SUB)
    extra = half - LANES
    for k in range(BLOCKS):
        gram[k, :, :LANES] = packed_ref[pitch * k : pitch * k + half]
        gram[k, :, LANES:] = packed_ref[
            pitch * BLOCKS : pitch * BLOCKS + half, extra * k : extra * k + extra
        ]
    for w in windows:
        held[w, 0] = start_ref[:half]
        held[w, 1] = start_ref[half:]

    def step(_, carry):
        images = []
        for w in windows:
            top, cross, low = gram[2 * w], gram[2 * w + 1], gram[2 * w + 2]
            above, below = held[w, 0], held[w, 1]
            images.append(
                (
                    dot(top, above, 1, 0) + dot(cross, below, 1, 0),
                    dot(cross, above, 0, 0) + dot(low, below, 1, 0),
                )
            )
        inverses = inverse_factors([dot(a, a, 0, 0) + dot(b, b, 0, 0) for a, b in images])
        for w in windows:
            for h in range(2):
                held[w, h] = dot(images[w][h], inverses[w], 1, 1)
        return carry

    lax.fori_loop(0, ITERS, step, 0)
    columns = lax.broadcasted_iota(jnp.int32, (1, K), 1)
    for w in windows:
        keep = ((columns >= low_ref[w]) & (columns < high_ref[w])).astype(jnp.float32)
        basis_ref[w, :half] = held[w, 0]
        basis_ref[w, half:] = held[w, 1]
        for i in range(2):
            for j in range(2):
                proj_ref[w, i, j] = dot(held[w, i] * keep, held[w, j], 1, 1).astype(jnp.bfloat16)


def iterate(packed, start, low, high):
    half = start.shape[0] // 2
    return pl.pallas_call(
        functools.partial(iterate_kernel, half),
        out_shape=(
            jax.ShapeDtypeStruct((WIN_DEV, 2 * half, K), jnp.float32),
            jax.ShapeDtypeStruct((WIN_DEV, 2, 2, half, half), jnp.bfloat16),
        ),
        in_specs=[SMEM, SMEM, VMEM, VMEM],
        out_specs=(VMEM, VMEM),
        scratch_shapes=[
            pltpu.VMEM((BLOCKS, half, half), jnp.float32),
            pltpu.VMEM((WIN_DEV, 2, half, K), jnp.float32),
        ],
        name="iterate",
    )(low, high, packed, start)


def filter_kernel(half, proj_ref, *refs):
    own, following, power_ref = refs[:2], refs[2:4], refs[4]
    for w in range(WIN_DEV):
        total = 0.0
        for part in range(2):
            above = own[part][w]
            below = own[part][1] if w == 0 else following[part][...]
            for i in range(2):
                rows = dot(proj_ref[w, i, 0], above, 1, 0, None)
                rows += dot(proj_ref[w, i, 1], below, 1, 0, None)
                total += jnp.sum(rows * rows, axis=0, keepdims=True)
        power_ref[w : w + 1] = total / (2 * half)


def filtered_power(projs, own, following):
    _, half, columns = own.shape
    pixels = columns // 2
    tile = 512
    count = pixels // tile
    return pl.pallas_call(
        functools.partial(filter_kernel, half),
        out_shape=jax.ShapeDtypeStruct((WIN_DEV, pixels), jnp.float32),
        grid=(count,),
        in_specs=[
            pl.BlockSpec(projs.shape, lambda i: (0, 0, 0, 0, 0)),
            pl.BlockSpec((2, half, tile), lambda i: (0, 0, i)),
            pl.BlockSpec((2, half, tile), lambda i: (0, 0, i + count)),
            pl.BlockSpec((half, tile), lambda i: (0, i)),
            pl.BlockSpec((half, tile), lambda i: (0, i + count)),
        ],
        out_specs=pl.BlockSpec((WIN_DEV, tile), lambda i: (0, i)),
        name="filter",
    )(projs, own, own, following, following)


def body(iq, tail_frames, start_basis, low_rank, high_rank):
    half = iq.shape[0] // WIN_DEV
    incoming = from_behind(iq[:half], "tm", -1)
    at_end = lax.axis_index("tm") == lax.axis_size("tm") - 1
    following = jnp.where(at_end, tail_frames, incoming).reshape(half, -1)
    own = iq.reshape(WIN_DEV, half, -1)
    rows = up(up(half, SUB) * (BLOCKS + 1), SUB * lax.axis_size("pix"))
    packed = sum_over_pix(gram_blocks(own, following, rows))
    bases, projs = iterate(packed, start_basis, low_rank, high_rank)
    return (filtered_power(projs, own, following), bases)


def solution(mesh):
    placed = (P("tm", None, "pix"), P(None, None, "pix"), P(), P("tm"), P("tm"))
    return jax.shard_map(
        body,
        mesh=mesh,
        in_specs=placed,
        out_specs=(P("tm", "pix"), P("tm", None, None)),
        check_vma=False,
    )
```

```python
import functools

import jax
import jax.numpy as jnp
from jax import lax
from jax.experimental import pallas as pl
from jax.experimental.pallas import tpu as pltpu
from jax.sharding import PartitionSpec as P

K = 128
ITERS = 3
WIN_DEV = 2
SUB = 8
LANES = 128
BLOCKS = 5
HI = lax.Precision.HIGHEST
MESH = pl.DeviceIdType.MESH
VMEM = pl.BlockSpec(memory_space=pltpu.VMEM)
SMEM = pl.BlockSpec(memory_space=pltpu.SMEM)


def dot(a, b, ca, cb, precision=HI):
    return lax.dot_general(
        a, b, (((ca,), (cb,)), ((), ())), precision=precision, preferred_element_type=jnp.float32
    )


def up(value, unit):
    return -(-value // unit) * unit


def gram_kernel(half, own_ref, next_ref, packed_ref, acc):
    step = pl.program_id(0)

    @pl.when(step == 0)
    def _():
        acc[...] = jnp.zeros_like(acc)

    first, second, third = own_ref[0], own_ref[1], next_ref[...]
    pairs = ((first, first), (first, second), (second, second), (second, third), (third, third))
    for k, (a, b) in enumerate(pairs):
        acc[k] += dot(a, b, 1, 1, None)

    @pl.when(step == pl.num_programs(0) - 1)
    def _():
        pitch = up(half, SUB)
        packed_ref[...] = jnp.zeros_like(packed_ref)
        for k in range(BLOCKS):
            packed_ref[pitch * k : pitch * k + half] = acc[k, :, :LANES]
        rest = [acc[k, :, LANES:] for k in range(BLOCKS)]
        rest.append(jnp.zeros((half, LANES - BLOCKS * (half - LANES)), jnp.float32))
        packed_ref[pitch * BLOCKS : pitch * BLOCKS + half] = jnp.concatenate(rest, axis=1)


def gram_blocks(own, following, rows):
    _, half, columns = own.shape
    tile = 1024
    return pl.pallas_call(
        functools.partial(gram_kernel, half),
        out_shape=jax.ShapeDtypeStruct((rows, LANES), jnp.float32),
        grid=(columns // tile,),
        in_specs=[
            pl.BlockSpec((2, half, tile), lambda i: (0, 0, i)),
            pl.BlockSpec((half, tile), lambda i: (0, i)),
        ],
        out_specs=pl.BlockSpec((rows, LANES), lambda i: (0, 0)),
        scratch_shapes=[pltpu.VMEM((BLOCKS, half, half), jnp.float32)],
        name="gram",
    )(own, following)


def cross_kernel(half, place_ref, own_ref, swapped_ref, packed_ref, extra_ref, acc):
    step = pl.program_id(0)

    @pl.when(step == 0)
    def _():
        acc[...] = jnp.zeros_like(acc)

    front = place_ref[0] == 0
    mine, theirs = own_ref[0], swapped_ref[...]
    acc[...] += dot(
        jnp.where(front, mine, theirs), jnp.where(front, theirs, mine), 1, 1, None
    )

    @pl.when(step == pl.num_programs(0) - 1)
    def _():
        pitch = up(half, SUB)
        rest = half - LANES
        extra_ref[...] = jnp.zeros_like(extra_ref)
        extra_ref[:half] = acc[:, :LANES]
        extra_ref[pitch : pitch + half] = packed_ref[:half]
        extra_ref[2 * pitch : 2 * pitch + half] = jnp.concatenate(
            [
                jnp.zeros((half, 3 * rest), jnp.float32),
                acc[:, LANES:],
                packed_ref[pitch * BLOCKS : pitch * BLOCKS + half, :rest],
                jnp.zeros((half, LANES - BLOCKS * rest), jnp.float32),
            ],
            axis=1,
        )


def cross_block(place, own, swapped, packed):
    _, half, columns = own.shape
    tile = 1024
    count = columns // 2 // tile
    rows = 3 * up(half, SUB)
    return pl.pallas_call(
        functools.partial(cross_kernel, half),
        out_shape=jax.ShapeDtypeStruct((rows, LANES), jnp.float32),
        grid_spec=pltpu.PrefetchScalarGridSpec(
            num_scalar_prefetch=1,
            grid=(count,),
            in_specs=[
                pl.BlockSpec((1, half, tile), lambda i, t: (1 - t[0], 0, i + t[0] * count)),
                pl.BlockSpec((half, tile), lambda i, t: (0, i)),
                pl.BlockSpec(packed.shape, lambda i, t: (0, 0)),
            ],
            out_specs=pl.BlockSpec((rows, LANES), lambda i, t: (0, 0)),
            scratch_shapes=[pltpu.VMEM((half, half), jnp.float32)],
        ),
        name="cross",
    )(place, own, swapped, packed)


def sum_kernel(n, extra, x_ref, extra_ref, out_ref, whole, arrived, acc, landed, gathered, send_sem, recv_sem):
    me = lax.axis_index("pix")
    front = lax.axis_index("tm") == 0
    other = 1 - lax.axis_index("tm")
    bits = n.bit_length() - 1
    bit = [lax.rem(me // (1 << b), 2) for b in range(bits)]
    partner = [me + (1 - 2 * bit[b]) * (1 << b) for b in range(bits)]

    barrier = pltpu.get_barrier_semaphore()
    for b in range(bits):
        pl.semaphore_signal(
            barrier, inc=1, device_id={"pix": partner[b]}, device_id_type=MESH
        )
    pl.semaphore_signal(barrier, inc=1, device_id={"tm": other}, device_id_type=MESH)
    pl.semaphore_wait(barrier, bits + 1)

    copy = pltpu.make_async_remote_copy(
        src_ref=extra_ref,
        dst_ref=arrived,
        send_sem=send_sem.at[2 * bits],
        recv_sem=recv_sem.at[2 * bits],
        device_id={"tm": other},
        device_id_type=MESH,
    )
    copy.start()
    pitch = extra_ref.shape[0] // 3
    cross, low, rest = pl.ds(0, pitch), pl.ds(pitch, pitch), pl.ds(2 * pitch, pitch)
    whole[pl.ds(0, 3 * pitch)] = x_ref[pl.ds(0, 3 * pitch)]
    tail = 6 * pitch
    whole[pl.ds(tail, x_ref.shape[0] - tail)] = x_ref[pl.ds(tail, x_ref.shape[0] - tail)]
    copy.wait()
    at = pl.ds(3 * pitch, pitch)
    whole[at] = jnp.where(front, extra_ref[cross] + arrived[cross], x_ref[at])
    at = pl.ds(4 * pitch, pitch)
    whole[at] = jnp.where(front, arrived[low], x_ref[at])
    at = pl.ds(5 * pitch, pitch)
    lane = lax.broadcasted_iota(jnp.int32, (pitch, LANES), 1)
    merged = jnp.where(lane < 3 * extra, x_ref[at], arrived[rest])
    merged += jnp.where((lane >= 3 * extra) & (lane < 4 * extra), extra_ref[rest], 0.0)
    whole[at] = jnp.where(front, merged, x_ref[at])

    def window(start, size):
        return pl.ds(pl.multiple_of(start, SUB), size)

    start, size, base = 0, x_ref.shape[0], 0
    for b in range(bits):
        size //= 2
        keep = start + bit[b] * size
        give = start + (1 - bit[b]) * size
        source = whole if b == 0 else acc
        copy = pltpu.make_async_remote_copy(
            src_ref=source.at[window(give, size)],
            dst_ref=landed.at[pl.ds(base, size)],
            send_sem=send_sem.at[b],
            recv_sem=recv_sem.at[b],
            device_id={"pix": partner[b]},
            device_id_type=MESH,
        )
        copy.start()
        copy.wait()
        target = gathered if b == bits - 1 else acc
        target[window(keep, size)] = source[window(keep, size)] + landed[pl.ds(base, size)]
        start, base = keep, base + size
    for b in reversed(range(bits)):
        copy = pltpu.make_async_remote_copy(
            src_ref=gathered.at[window(start, size)],
            dst_ref=gathered.at[window(start, size)],
            send_sem=send_sem.at[bits + b],
            recv_sem=recv_sem.at[bits + b],
            device_id={"pix": partner[b]},
            device_id_type=MESH,
        )
        copy.start()
        copy.wait()
        start, size = start - bit[b] * size, 2 * size
    out_ref[...] = gathered[...]


def sum_over_pix(packed, crossing, half):
    n = lax.axis_size("pix")
    bits = n.bit_length() - 1
    return pl.pallas_call(
        functools.partial(sum_kernel, n, half - LANES),
        out_shape=jax.ShapeDtypeStruct(packed.shape, jnp.float32),
        in_specs=[VMEM, VMEM],
        out_specs=VMEM,
        scratch_shapes=[
            pltpu.VMEM(packed.shape, jnp.float32),
            pltpu.VMEM(crossing.shape, jnp.float32),
            pltpu.VMEM(packed.shape, jnp.float32),
            pltpu.VMEM(packed.shape, jnp.float32),
            pltpu.VMEM(packed.shape, jnp.float32),
            pltpu.SemaphoreType.DMA((2 * bits + 1,)),
            pltpu.SemaphoreType.DMA((2 * bits + 1,)),
        ],
        compiler_params=pltpu.CompilerParams(collective_id=0, has_side_effects=True),
        name="sum_over_pix",
    )(packed, crossing)


def inverse_factors(grams):
    tiles = K // SUB
    lane = lax.broadcasted_iota(jnp.int32, (SUB, K), 1)
    sub = lax.broadcasted_iota(jnp.int32, (SUB, K), 0)
    work = [[m[SUB * u : SUB * u + SUB, :] for u in range(tiles)] for m in grams]
    for j in range(K):
        t, s = divmod(j, SUB)
        here = lane == j
        for rows in work:
            pivot = rows[t][s : s + 1, j : j + 1]
            scaled = jnp.where(here[:1], 1.0, rows[t][s : s + 1, :]) * (1.0 / pivot)
            for u in range(t, tiles):
                if u == t and s == SUB - 1:
                    continue
                column = rows[u][:, j : j + 1]
                update = jnp.where(here, 0.0, rows[u]) - column * scaled
                rows[u] = jnp.where(sub > s, update, rows[u]) if u == t else update
    inverses = []
    for rows in work:
        out = []
        for u in range(tiles):
            row = sub + SUB * u
            diagonal = jnp.sum(jnp.where(lane == row, rows[u], 0.0), axis=1, keepdims=True)
            unit = jnp.where(lane < row, rows[u], jnp.where(lane == row, 1.0, 0.0))
            out.append(unit * lax.rsqrt(diagonal))
        inverses.append(jnp.concatenate(out, axis=0))
    return inverses


def iterate_kernel(half, low_ref, high_ref, packed_ref, start_ref, basis_ref, proj_ref, gram, held):
    windows = range(WIN_DEV)
    pitch = up(half, SUB)
    extra = half - LANES
    for k in range(BLOCKS):
        gram[k, :, :LANES] = packed_ref[pitch * k : pitch * k + half]
        gram[k, :, LANES:] = packed_ref[
            pitch * BLOCKS : pitch * BLOCKS + half, extra * k : extra * k + extra
        ]
    for w in windows:
        held[w, 0] = start_ref[:half]
        held[w, 1] = start_ref[half:]

    def step(_, carry):
        images = []
        for w in windows:
            top, cross, low = gram[2 * w], gram[2 * w + 1], gram[2 * w + 2]
            above, below = held[w, 0], held[w, 1]
            images.append(
                (
                    dot(top, above, 1, 0) + dot(cross, below, 1, 0),
                    dot(cross, above, 0, 0) + dot(low, below, 1, 0),
                )
            )
        inverses = inverse_factors([dot(a, a, 0, 0) + dot(b, b, 0, 0) for a, b in images])
        for w in windows:
            for h in range(2):
                held[w, h] = dot(images[w][h], inverses[w], 1, 1)
        return carry

    lax.fori_loop(0, ITERS, step, 0)
    columns = lax.broadcasted_iota(jnp.int32, (1, K), 1)
    for w in windows:
        keep = ((columns >= low_ref[w]) & (columns < high_ref[w])).astype(jnp.float32)
        basis_ref[w, :half] = held[w, 0]
        basis_ref[w, half:] = held[w, 1]
        for i in range(2):
            for j in range(2):
                proj_ref[w, i, j] = dot(held[w, i] * keep, held[w, j], 1, 1).astype(jnp.bfloat16)


def iterate(packed, start, low, high):
    half = start.shape[0] // 2
    return pl.pallas_call(
        functools.partial(iterate_kernel, half),
        out_shape=(
            jax.ShapeDtypeStruct((WIN_DEV, 2 * half, K), jnp.float32),
            jax.ShapeDtypeStruct((WIN_DEV, 2, 2, half, half), jnp.bfloat16),
        ),
        in_specs=[SMEM, SMEM, VMEM, VMEM],
        out_specs=(VMEM, VMEM),
        scratch_shapes=[
            pltpu.VMEM((BLOCKS, half, half), jnp.float32),
            pltpu.VMEM((WIN_DEV, 2, half, K), jnp.float32),
        ],
        cost_estimate=pl.CostEstimate(flops=40_000_000_000, bytes_accessed=1_000_000, transcendentals=0),
        name="iterate",
    )(low, high, packed, start)


def filter_kernel(half, place_ref, proj_ref, *refs):
    own, arrived, tail, power_ref = refs[:2], refs[2:4], refs[4:6], refs[6]
    front = place_ref[0] == 0
    for w in range(WIN_DEV):
        total = 0.0
        for part in range(2):
            above = own[part][w]
            if w == 0:
                below = own[part][1]
            else:
                below = jnp.where(front, arrived[part][...], tail[part][...])
            for i in range(2):
                rows = dot(proj_ref[w, i, 0], above, 1, 0, None)
                rows += dot(proj_ref[w, i, 1], below, 1, 0, None)
                total += jnp.sum(rows * rows, axis=0, keepdims=True)
        power_ref[w : w + 1] = total / (2 * half)


def filtered_power(place, projs, own, arrived, tail):
    _, half, columns = own.shape
    pixels = columns // 2
    tile = 512
    count = pixels // tile
    return pl.pallas_call(
        functools.partial(filter_kernel, half),
        out_shape=jax.ShapeDtypeStruct((WIN_DEV, pixels), jnp.float32),
        grid=(count,),
        in_specs=[
            SMEM,
            pl.BlockSpec(projs.shape, lambda i: (0, 0, 0, 0, 0)),
            pl.BlockSpec((2, half, tile), lambda i: (0, 0, i)),
            pl.BlockSpec((2, half, tile), lambda i: (0, 0, i + count)),
            pl.BlockSpec((half, tile), lambda i: (0, i)),
            pl.BlockSpec((half, tile), lambda i: (0, i)),
            pl.BlockSpec((half, tile), lambda i: (0, i)),
            pl.BlockSpec((half, tile), lambda i: (0, i + count)),
        ],
        out_specs=pl.BlockSpec((WIN_DEV, tile), lambda i: (0, i)),
        name="filter",
    )(place, projs, own, own, *arrived, tail, tail)


def body(iq, tail_frames, start_basis, low_rank, high_rank):
    assert lax.axis_size("tm") == 2
    half = iq.shape[0] // WIN_DEV
    place = lax.axis_index("tm")
    front = place == 0
    place = place.reshape(1).astype(jnp.int32)
    swapped = lax.ppermute(
        jnp.where(front, iq[half:, 1], iq[:half, 0]), "tm", [(0, 1), (1, 0)]
    )
    own = iq.reshape(WIN_DEV, half, -1)
    tail = tail_frames.reshape(half, -1)
    rows = up(up(half, SUB) * (BLOCKS + 1), SUB * lax.axis_size("pix"))
    packed = gram_blocks(own, tail, rows)
    crossing = cross_block(place, own, swapped, packed)
    summed = sum_over_pix(packed, crossing, half)
    late, summed = lax.optimization_barrier((iq[:half, 1], summed))
    late = lax.ppermute(late, "tm", [(1, 0)])
    bases, projs = iterate(summed, start_basis, low_rank, high_rank)
    return (filtered_power(place, projs, own, (swapped, late), tail), bases)


def solution(mesh):
    placed = (P("tm", None, "pix"), P(None, None, "pix"), P(), P("tm"), P("tm"))
    return jax.shard_map(
        body,
        mesh=mesh,
        in_specs=placed,
        out_specs=(P("tm", "pix"), P("tm", None, None)),
        check_vma=False,
    )
```

```python
import functools

import jax
import jax.numpy as jnp
from jax import lax
from jax.experimental import pallas as pl
from jax.experimental.pallas import tpu as pltpu
from jax.sharding import PartitionSpec as P

K = 128
ITERS = 3
WIN_DEV = 2
SUB = 8
PANEL = 4
LANES = 128
BLOCKS = 5
HI = lax.Precision.HIGHEST
MESH = pl.DeviceIdType.MESH
VMEM = pl.BlockSpec(memory_space=pltpu.VMEM)
SMEM = pl.BlockSpec(memory_space=pltpu.SMEM)


def dot(a, b, ca, cb, precision=HI):
    return lax.dot_general(
        a, b, (((ca,), (cb,)), ((), ())), precision=precision, preferred_element_type=jnp.float32
    )


def up(value, unit):
    return -(-value // unit) * unit


def gram_kernel(half, own_ref, next_ref, packed_ref, acc):
    step = pl.program_id(0)

    @pl.when(step == 0)
    def _():
        acc[...] = jnp.zeros_like(acc)

    first, second, third = own_ref[0], own_ref[1], next_ref[...]
    pairs = ((first, first), (first, second), (second, second), (second, third), (third, third))
    for k, (a, b) in enumerate(pairs):
        acc[k] += dot(a, b, 1, 1, None)

    @pl.when(step == pl.num_programs(0) - 1)
    def _():
        pitch = up(half, SUB)
        packed_ref[...] = jnp.zeros_like(packed_ref)
        for k in range(BLOCKS):
            packed_ref[pitch * k : pitch * k + half] = acc[k, :, :LANES]
        rest = [acc[k, :, LANES:] for k in range(BLOCKS)]
        rest.append(jnp.zeros((half, LANES - BLOCKS * (half - LANES)), jnp.float32))
        packed_ref[pitch * BLOCKS : pitch * BLOCKS + half] = jnp.concatenate(rest, axis=1)


def gram_blocks(own, following, rows):
    _, half, columns = own.shape
    tile = 1024
    return pl.pallas_call(
        functools.partial(gram_kernel, half),
        out_shape=jax.ShapeDtypeStruct((rows, LANES), jnp.float32),
        grid=(columns // tile,),
        in_specs=[
            pl.BlockSpec((2, half, tile), lambda i: (0, 0, i)),
            pl.BlockSpec((half, tile), lambda i: (0, i)),
        ],
        out_specs=pl.BlockSpec((rows, LANES), lambda i: (0, 0)),
        scratch_shapes=[pltpu.VMEM((BLOCKS, half, half), jnp.float32)],
        name="gram",
    )(own, following)


def cross_kernel(half, place_ref, own_ref, swapped_ref, packed_ref, extra_ref, acc):
    step = pl.program_id(0)

    @pl.when(step == 0)
    def _():
        acc[...] = jnp.zeros_like(acc)

    front = place_ref[0] == 0
    mine, theirs = own_ref[0], swapped_ref[...]
    acc[...] += dot(
        jnp.where(front, mine, theirs), jnp.where(front, theirs, mine), 1, 1, None
    )

    @pl.when(step == pl.num_programs(0) - 1)
    def _():
        pitch = up(half, SUB)
        rest = half - LANES
        extra_ref[...] = jnp.zeros_like(extra_ref)
        extra_ref[:half] = acc[:, :LANES]
        extra_ref[pitch : pitch + half] = packed_ref[:half]
        extra_ref[2 * pitch : 2 * pitch + half] = jnp.concatenate(
            [
                jnp.zeros((half, 3 * rest), jnp.float32),
                acc[:, LANES:],
                packed_ref[pitch * BLOCKS : pitch * BLOCKS + half, :rest],
                jnp.zeros((half, LANES - BLOCKS * rest), jnp.float32),
            ],
            axis=1,
        )


def cross_block(place, own, swapped, packed):
    _, half, columns = own.shape
    tile = 1024
    count = columns // 2 // tile
    rows = 3 * up(half, SUB)
    return pl.pallas_call(
        functools.partial(cross_kernel, half),
        out_shape=jax.ShapeDtypeStruct((rows, LANES), jnp.float32),
        grid_spec=pltpu.PrefetchScalarGridSpec(
            num_scalar_prefetch=1,
            grid=(count,),
            in_specs=[
                pl.BlockSpec((1, half, tile), lambda i, t: (1 - t[0], 0, i + t[0] * count)),
                pl.BlockSpec((half, tile), lambda i, t: (0, i)),
                pl.BlockSpec(packed.shape, lambda i, t: (0, 0)),
            ],
            out_specs=pl.BlockSpec((rows, LANES), lambda i, t: (0, 0)),
            scratch_shapes=[pltpu.VMEM((half, half), jnp.float32)],
        ),
        name="cross",
    )(place, own, swapped, packed)


def sum_kernel(n, extra, x_ref, extra_ref, out_ref, whole, arrived, acc, landed, gathered, send_sem, recv_sem):
    me = lax.axis_index("pix")
    front = lax.axis_index("tm") == 0
    other = 1 - lax.axis_index("tm")
    bits = n.bit_length() - 1
    bit = [lax.rem(me // (1 << b), 2) for b in range(bits)]
    partner = [me + (1 - 2 * bit[b]) * (1 << b) for b in range(bits)]

    barrier = pltpu.get_barrier_semaphore()
    for b in range(bits):
        pl.semaphore_signal(
            barrier, inc=1, device_id={"pix": partner[b]}, device_id_type=MESH
        )
    pl.semaphore_signal(barrier, inc=1, device_id={"tm": other}, device_id_type=MESH)
    pl.semaphore_wait(barrier, bits + 1)

    copy = pltpu.make_async_remote_copy(
        src_ref=extra_ref,
        dst_ref=arrived,
        send_sem=send_sem.at[2 * bits],
        recv_sem=recv_sem.at[2 * bits],
        device_id={"tm": other},
        device_id_type=MESH,
    )
    copy.start()
    pitch = extra_ref.shape[0] // 3
    cross, low, rest = pl.ds(0, pitch), pl.ds(pitch, pitch), pl.ds(2 * pitch, pitch)
    whole[pl.ds(0, 3 * pitch)] = x_ref[pl.ds(0, 3 * pitch)]
    tail = 6 * pitch
    whole[pl.ds(tail, x_ref.shape[0] - tail)] = x_ref[pl.ds(tail, x_ref.shape[0] - tail)]
    copy.wait()
    at = pl.ds(3 * pitch, pitch)
    whole[at] = jnp.where(front, extra_ref[cross] + arrived[cross], x_ref[at])
    at = pl.ds(4 * pitch, pitch)
    whole[at] = jnp.where(front, arrived[low], x_ref[at])
    at = pl.ds(5 * pitch, pitch)
    lane = lax.broadcasted_iota(jnp.int32, (pitch, LANES), 1)
    merged = jnp.where(lane < 3 * extra, x_ref[at], arrived[rest])
    merged += jnp.where((lane >= 3 * extra) & (lane < 4 * extra), extra_ref[rest], 0.0)
    whole[at] = jnp.where(front, merged, x_ref[at])

    def window(start, size):
        return pl.ds(pl.multiple_of(start, SUB), size)

    start, size, base = 0, x_ref.shape[0], 0
    for b in range(bits):
        size //= 2
        keep = start + bit[b] * size
        give = start + (1 - bit[b]) * size
        source = whole if b == 0 else acc
        copy = pltpu.make_async_remote_copy(
            src_ref=source.at[window(give, size)],
            dst_ref=landed.at[pl.ds(base, size)],
            send_sem=send_sem.at[b],
            recv_sem=recv_sem.at[b],
            device_id={"pix": partner[b]},
            device_id_type=MESH,
        )
        copy.start()
        copy.wait()
        target = gathered if b == bits - 1 else acc
        target[window(keep, size)] = source[window(keep, size)] + landed[pl.ds(base, size)]
        start, base = keep, base + size
    for b in reversed(range(bits)):
        copy = pltpu.make_async_remote_copy(
            src_ref=gathered.at[window(start, size)],
            dst_ref=gathered.at[window(start, size)],
            send_sem=send_sem.at[bits + b],
            recv_sem=recv_sem.at[bits + b],
            device_id={"pix": partner[b]},
            device_id_type=MESH,
        )
        copy.start()
        copy.wait()
        start, size = start - bit[b] * size, 2 * size
    out_ref[...] = gathered[...]


def sum_over_pix(packed, crossing, half):
    n = lax.axis_size("pix")
    bits = n.bit_length() - 1
    return pl.pallas_call(
        functools.partial(sum_kernel, n, half - LANES),
        out_shape=jax.ShapeDtypeStruct(packed.shape, jnp.float32),
        in_specs=[VMEM, VMEM],
        out_specs=VMEM,
        scratch_shapes=[
            pltpu.VMEM(packed.shape, jnp.float32),
            pltpu.VMEM(crossing.shape, jnp.float32),
            pltpu.VMEM(packed.shape, jnp.float32),
            pltpu.VMEM(packed.shape, jnp.float32),
            pltpu.VMEM(packed.shape, jnp.float32),
            pltpu.SemaphoreType.DMA((2 * bits + 1,)),
            pltpu.SemaphoreType.DMA((2 * bits + 1,)),
        ],
        compiler_params=pltpu.CompilerParams(collective_id=0, has_side_effects=True),
        name="sum_over_pix",
    )(packed, crossing)


def inverse_factors(grams):
    tiles = K // SUB
    lane = lax.broadcasted_iota(jnp.int32, (SUB, K), 1)
    sub = lax.broadcasted_iota(jnp.int32, (SUB, K), 0)
    work = [[m[SUB * u : SUB * u + SUB, :] for u in range(tiles)] for m in grams]
    for start in range(0, K, PANEL):
        t = start // SUB
        for rows in work:
            spread = [
                {
                    u: jnp.broadcast_to(rows[u][:, start + p : start + p + 1], (SUB, K))
                    for u in range(t, tiles)
                }
                for p in range(PANEL)
            ]
            for p in range(PANEL):
                s = (start + p) % SUB
                here = lane == start + p
                inverse = 1.0 / spread[p][t][s : s + 1, :]
                scaled = jnp.where(here[:1], 1.0, rows[t][s : s + 1, :]) * inverse
                factors = [spread[q][t][s : s + 1, :] * inverse for q in range(p + 1, PANEL)]
                for u in range(t, tiles):
                    if u == t and s == SUB - 1:
                        continue
                    column = spread[p][u]
                    for q, factor in zip(range(p + 1, PANEL), factors):
                        update = spread[q][u] - column * factor
                        spread[q][u] = jnp.where(sub > s, update, spread[q][u]) if u == t else update
                    update = jnp.where(here, 0.0, rows[u]) - column * scaled
                    rows[u] = jnp.where(sub > s, update, rows[u]) if u == t else update
    inverses = []
    for rows in work:
        out = []
        for u in range(tiles):
            row = sub + SUB * u
            diagonal = jnp.sum(jnp.where(lane == row, rows[u], 0.0), axis=1, keepdims=True)
            unit = jnp.where(lane < row, rows[u], jnp.where(lane == row, 1.0, 0.0))
            out.append(unit * lax.rsqrt(diagonal))
        inverses.append(jnp.concatenate(out, axis=0))
    return inverses


def iterate_kernel(half, low_ref, high_ref, packed_ref, start_ref, basis_ref, proj_ref, gram, held):
    windows = range(WIN_DEV)
    pitch = up(half, SUB)
    extra = half - LANES
    for k in range(BLOCKS):
        gram[k, :, :LANES] = packed_ref[pitch * k : pitch * k + half]
        gram[k, :, LANES:] = packed_ref[
            pitch * BLOCKS : pitch * BLOCKS + half, extra * k : extra * k + extra
        ]
    for w in windows:
        held[w, 0] = start_ref[:half]
        held[w, 1] = start_ref[half:]

    def step(_, carry):
        images = []
        for w in windows:
            top, cross, low = gram[2 * w], gram[2 * w + 1], gram[2 * w + 2]
            above, below = held[w, 0], held[w, 1]
            images.append(
                (
                    dot(top, above, 1, 0) + dot(cross, below, 1, 0),
                    dot(cross, above, 0, 0) + dot(low, below, 1, 0),
                )
            )
        inverses = inverse_factors([dot(a, a, 0, 0) + dot(b, b, 0, 0) for a, b in images])
        for w in windows:
            for h in range(2):
                held[w, h] = dot(images[w][h], inverses[w], 1, 1)
        return carry

    lax.fori_loop(0, ITERS, step, 0)
    columns = lax.broadcasted_iota(jnp.int32, (1, K), 1)
    for w in windows:
        keep = ((columns >= low_ref[w]) & (columns < high_ref[w])).astype(jnp.float32)
        basis_ref[w, :half] = held[w, 0]
        basis_ref[w, half:] = held[w, 1]
        for i in range(2):
            for j in range(2):
                proj_ref[w, i, j] = dot(held[w, i] * keep, held[w, j], 1, 1).astype(jnp.bfloat16)


def iterate(packed, start, low, high):
    half = start.shape[0] // 2
    return pl.pallas_call(
        functools.partial(iterate_kernel, half),
        out_shape=(
            jax.ShapeDtypeStruct((WIN_DEV, 2 * half, K), jnp.float32),
            jax.ShapeDtypeStruct((WIN_DEV, 2, 2, half, half), jnp.bfloat16),
        ),
        in_specs=[SMEM, SMEM, VMEM, VMEM],
        out_specs=(VMEM, VMEM),
        scratch_shapes=[
            pltpu.VMEM((BLOCKS, half, half), jnp.float32),
            pltpu.VMEM((WIN_DEV, 2, half, K), jnp.float32),
        ],
        cost_estimate=pl.CostEstimate(flops=40_000_000_000, bytes_accessed=1_000_000, transcendentals=0),
        name="iterate",
    )(low, high, packed, start)


def filter_kernel(half, place_ref, proj_ref, *refs):
    own, arrived, tail, power_ref = refs[:2], refs[2:4], refs[4:6], refs[6]
    front = place_ref[0] == 0
    for w in range(WIN_DEV):
        total = 0.0
        for part in range(2):
            above = own[part][w]
            if w == 0:
                below = own[part][1]
            else:
                below = jnp.where(front, arrived[part][...], tail[part][...])
            for i in range(2):
                rows = dot(proj_ref[w, i, 0], above, 1, 0, None)
                rows += dot(proj_ref[w, i, 1], below, 1, 0, None)
                total += jnp.sum(rows * rows, axis=0, keepdims=True)
        power_ref[w : w + 1] = total / (2 * half)


def filtered_power(place, projs, own, arrived, tail):
    _, half, columns = own.shape
    pixels = columns // 2
    tile = 512
    count = pixels // tile
    return pl.pallas_call(
        functools.partial(filter_kernel, half),
        out_shape=jax.ShapeDtypeStruct((WIN_DEV, pixels), jnp.float32),
        grid=(count,),
        in_specs=[
            SMEM,
            pl.BlockSpec(projs.shape, lambda i: (0, 0, 0, 0, 0)),
            pl.BlockSpec((2, half, tile), lambda i: (0, 0, i)),
            pl.BlockSpec((2, half, tile), lambda i: (0, 0, i + count)),
            pl.BlockSpec((half, tile), lambda i: (0, i)),
            pl.BlockSpec((half, tile), lambda i: (0, i)),
            pl.BlockSpec((half, tile), lambda i: (0, i)),
            pl.BlockSpec((half, tile), lambda i: (0, i + count)),
        ],
        out_specs=pl.BlockSpec((WIN_DEV, tile), lambda i: (0, i)),
        name="filter",
    )(place, projs, own, own, *arrived, tail, tail)


def body(iq, tail_frames, start_basis, low_rank, high_rank):
    assert lax.axis_size("tm") == 2
    half = iq.shape[0] // WIN_DEV
    place = lax.axis_index("tm")
    front = place == 0
    place = place.reshape(1).astype(jnp.int32)
    own = iq.reshape(WIN_DEV, half, -1)
    middle = own.shape[2] // 2
    swapped = lax.ppermute(
        jnp.where(front, own[1, :, middle:], own[0, :, :middle]), "tm", [(0, 1), (1, 0)]
    )
    tail = tail_frames.reshape(half, -1)
    rows = up(up(half, SUB) * (BLOCKS + 1), SUB * lax.axis_size("pix"))
    packed = gram_blocks(own, tail, rows)
    crossing = cross_block(place, own, swapped, packed)
    summed = sum_over_pix(packed, crossing, half)
    late, summed = lax.optimization_barrier((own[0, :, middle:], summed))
    late = lax.ppermute(late, "tm", [(1, 0)])
    bases, projs = iterate(summed, start_basis, low_rank, high_rank)
    return (filtered_power(place, projs, own, (swapped, late), tail), bases)


def solution(mesh):
    placed = (P("tm", None, "pix"), P(None, None, "pix"), P(), P("tm"), P("tm"))
    return jax.shard_map(
        body,
        mesh=mesh,
        in_specs=placed,
        out_specs=(P("tm", "pix"), P("tm", None, None)),
        check_vma=False,
    )
```

```python
import functools

import jax
import jax.numpy as jnp
from jax import lax
from jax.experimental import pallas as pl
from jax.experimental.pallas import tpu as pltpu
from jax.sharding import PartitionSpec as P

K = 128
ITERS = 3
WIN_DEV = 2
SUB = 8
PANEL = 8
LANES = 128
BLOCKS = 5
HI = lax.Precision.HIGHEST
MESH = pl.DeviceIdType.MESH
VMEM = pl.BlockSpec(memory_space=pltpu.VMEM)
SMEM = pl.BlockSpec(memory_space=pltpu.SMEM)


def dot(a, b, ca, cb, precision=HI):
    return lax.dot_general(
        a, b, (((ca,), (cb,)), ((), ())), precision=precision, preferred_element_type=jnp.float32
    )


def up(value, unit):
    return -(-value // unit) * unit


def gram_kernel(half, own_ref, next_ref, packed_ref, acc):
    step = pl.program_id(0)

    @pl.when(step == 0)
    def _():
        acc[...] = jnp.zeros_like(acc)

    first, second, third = own_ref[0], own_ref[1], next_ref[...]
    pairs = ((first, first), (first, second), (second, second), (second, third), (third, third))
    for k, (a, b) in enumerate(pairs):
        acc[k] += dot(a, b, 1, 1, None)

    @pl.when(step == pl.num_programs(0) - 1)
    def _():
        pitch = up(half, SUB)
        packed_ref[...] = jnp.zeros_like(packed_ref)
        for k in range(BLOCKS):
            packed_ref[pitch * k : pitch * k + half] = acc[k, :, :LANES]
        rest = [acc[k, :, LANES:] for k in range(BLOCKS)]
        rest.append(jnp.zeros((half, LANES - BLOCKS * (half - LANES)), jnp.float32))
        packed_ref[pitch * BLOCKS : pitch * BLOCKS + half] = jnp.concatenate(rest, axis=1)


def gram_blocks(own, following, rows):
    _, half, columns = own.shape
    tile = 1024
    return pl.pallas_call(
        functools.partial(gram_kernel, half),
        out_shape=jax.ShapeDtypeStruct((rows, LANES), jnp.float32),
        grid=(columns // tile,),
        in_specs=[
            pl.BlockSpec((2, half, tile), lambda i: (0, 0, i)),
            pl.BlockSpec((half, tile), lambda i: (0, i)),
        ],
        out_specs=pl.BlockSpec((rows, LANES), lambda i: (0, 0)),
        scratch_shapes=[pltpu.VMEM((BLOCKS, half, half), jnp.float32)],
        name="gram",
    )(own, following)


def cross_kernel(half, place_ref, own_ref, swapped_ref, packed_ref, extra_ref, acc):
    step = pl.program_id(0)

    @pl.when(step == 0)
    def _():
        acc[...] = jnp.zeros_like(acc)

    front = place_ref[0] == 0
    mine, theirs = own_ref[0], swapped_ref[...]
    acc[...] += dot(
        jnp.where(front, mine, theirs), jnp.where(front, theirs, mine), 1, 1, None
    )

    @pl.when(step == pl.num_programs(0) - 1)
    def _():
        pitch = up(half, SUB)
        rest = half - LANES
        extra_ref[...] = jnp.zeros_like(extra_ref)
        extra_ref[:half] = acc[:, :LANES]
        extra_ref[pitch : pitch + half] = packed_ref[:half]
        extra_ref[2 * pitch : 2 * pitch + half] = jnp.concatenate(
            [
                jnp.zeros((half, 3 * rest), jnp.float32),
                acc[:, LANES:],
                packed_ref[pitch * BLOCKS : pitch * BLOCKS + half, :rest],
                jnp.zeros((half, LANES - BLOCKS * rest), jnp.float32),
            ],
            axis=1,
        )


def cross_block(place, own, swapped, packed):
    _, half, columns = own.shape
    tile = 1024
    count = columns // 2 // tile
    rows = 3 * up(half, SUB)
    return pl.pallas_call(
        functools.partial(cross_kernel, half),
        out_shape=jax.ShapeDtypeStruct((rows, LANES), jnp.float32),
        grid_spec=pltpu.PrefetchScalarGridSpec(
            num_scalar_prefetch=1,
            grid=(count,),
            in_specs=[
                pl.BlockSpec((1, half, tile), lambda i, t: (1 - t[0], 0, i + t[0] * count)),
                pl.BlockSpec((half, tile), lambda i, t: (0, i)),
                pl.BlockSpec(packed.shape, lambda i, t: (0, 0)),
            ],
            out_specs=pl.BlockSpec((rows, LANES), lambda i, t: (0, 0)),
            scratch_shapes=[pltpu.VMEM((half, half), jnp.float32)],
        ),
        name="cross",
    )(place, own, swapped, packed)


def sum_kernel(n, extra, x_ref, extra_ref, out_ref, whole, arrived, acc, landed, gathered, send_sem, recv_sem):
    me = lax.axis_index("pix")
    front = lax.axis_index("tm") == 0
    other = 1 - lax.axis_index("tm")
    bits = n.bit_length() - 1
    bit = [lax.rem(me // (1 << b), 2) for b in range(bits)]
    partner = [me + (1 - 2 * bit[b]) * (1 << b) for b in range(bits)]

    barrier = pltpu.get_barrier_semaphore()
    for b in range(bits):
        pl.semaphore_signal(
            barrier, inc=1, device_id={"pix": partner[b]}, device_id_type=MESH
        )
    pl.semaphore_signal(barrier, inc=1, device_id={"tm": other}, device_id_type=MESH)
    pl.semaphore_wait(barrier, bits + 1)

    copy = pltpu.make_async_remote_copy(
        src_ref=extra_ref,
        dst_ref=arrived,
        send_sem=send_sem.at[2 * bits],
        recv_sem=recv_sem.at[2 * bits],
        device_id={"tm": other},
        device_id_type=MESH,
    )
    copy.start()
    pitch = extra_ref.shape[0] // 3
    cross, low, rest = pl.ds(0, pitch), pl.ds(pitch, pitch), pl.ds(2 * pitch, pitch)
    whole[pl.ds(0, 3 * pitch)] = x_ref[pl.ds(0, 3 * pitch)]
    tail = 6 * pitch
    whole[pl.ds(tail, x_ref.shape[0] - tail)] = x_ref[pl.ds(tail, x_ref.shape[0] - tail)]
    copy.wait()
    at = pl.ds(3 * pitch, pitch)
    whole[at] = jnp.where(front, extra_ref[cross] + arrived[cross], x_ref[at])
    at = pl.ds(4 * pitch, pitch)
    whole[at] = jnp.where(front, arrived[low], x_ref[at])
    at = pl.ds(5 * pitch, pitch)
    lane = lax.broadcasted_iota(jnp.int32, (pitch, LANES), 1)
    merged = jnp.where(lane < 3 * extra, x_ref[at], arrived[rest])
    merged += jnp.where((lane >= 3 * extra) & (lane < 4 * extra), extra_ref[rest], 0.0)
    whole[at] = jnp.where(front, merged, x_ref[at])

    def window(start, size):
        return pl.ds(pl.multiple_of(start, SUB), size)

    start, size, base = 0, x_ref.shape[0], 0
    for b in range(bits):
        size //= 2
        keep = start + bit[b] * size
        give = start + (1 - bit[b]) * size
        source = whole if b == 0 else acc
        copy = pltpu.make_async_remote_copy(
            src_ref=source.at[window(give, size)],
            dst_ref=landed.at[pl.ds(base, size)],
            send_sem=send_sem.at[b],
            recv_sem=recv_sem.at[b],
            device_id={"pix": partner[b]},
            device_id_type=MESH,
        )
        copy.start()
        copy.wait()
        target = gathered if b == bits - 1 else acc
        target[window(keep, size)] = source[window(keep, size)] + landed[pl.ds(base, size)]
        start, base = keep, base + size
    for b in reversed(range(bits)):
        copy = pltpu.make_async_remote_copy(
            src_ref=gathered.at[window(start, size)],
            dst_ref=gathered.at[window(start, size)],
            send_sem=send_sem.at[bits + b],
            recv_sem=recv_sem.at[bits + b],
            device_id={"pix": partner[b]},
            device_id_type=MESH,
        )
        copy.start()
        copy.wait()
        start, size = start - bit[b] * size, 2 * size
    out_ref[...] = gathered[...]


def sum_over_pix(packed, crossing, half):
    n = lax.axis_size("pix")
    bits = n.bit_length() - 1
    return pl.pallas_call(
        functools.partial(sum_kernel, n, half - LANES),
        out_shape=jax.ShapeDtypeStruct(packed.shape, jnp.float32),
        in_specs=[VMEM, VMEM],
        out_specs=VMEM,
        scratch_shapes=[
            pltpu.VMEM(packed.shape, jnp.float32),
            pltpu.VMEM(crossing.shape, jnp.float32),
            pltpu.VMEM(packed.shape, jnp.float32),
            pltpu.VMEM(packed.shape, jnp.float32),
            pltpu.VMEM(packed.shape, jnp.float32),
            pltpu.SemaphoreType.DMA((2 * bits + 1,)),
            pltpu.SemaphoreType.DMA((2 * bits + 1,)),
        ],
        compiler_params=pltpu.CompilerParams(collective_id=0, has_side_effects=True),
        name="sum_over_pix",
    )(packed, crossing)


def inverse_factors(grams):
    tiles = K // SUB
    lane = lax.broadcasted_iota(jnp.int32, (SUB, K), 1)
    sub = lax.broadcasted_iota(jnp.int32, (SUB, K), 0)
    work = [[m[SUB * u : SUB * u + SUB, :] for u in range(tiles)] for m in grams]
    for start in range(0, K, PANEL):
        t = start // SUB
        for rows in work:
            spread = [
                {
                    u: jnp.broadcast_to(rows[u][:, start + p : start + p + 1], (SUB, K))
                    for u in range(t, tiles)
                }
                for p in range(PANEL)
            ]
            for p in range(PANEL):
                s = (start + p) % SUB
                here = lane == start + p
                inverse = 1.0 / spread[p][t][s : s + 1, :]
                scaled = jnp.where(here[:1], 1.0, rows[t][s : s + 1, :]) * inverse
                factors = [spread[q][t][s : s + 1, :] * inverse for q in range(p + 1, PANEL)]
                for u in range(t, tiles):
                    if u == t and s == SUB - 1:
                        continue
                    column = spread[p][u]
                    for q, factor in zip(range(p + 1, PANEL), factors):
                        update = spread[q][u] - column * factor
                        spread[q][u] = jnp.where(sub > s, update, spread[q][u]) if u == t else update
                    update = jnp.where(here, 0.0, rows[u]) - column * scaled
                    rows[u] = jnp.where(sub > s, update, rows[u]) if u == t else update
    inverses = []
    for rows in work:
        out = []
        for u in range(tiles):
            row = sub + SUB * u
            diagonal = jnp.sum(jnp.where(lane == row, rows[u], 0.0), axis=1, keepdims=True)
            unit = jnp.where(lane < row, rows[u], jnp.where(lane == row, 1.0, 0.0))
            out.append(unit * lax.rsqrt(diagonal))
        inverses.append(jnp.concatenate(out, axis=0))
    return inverses


def iterate_kernel(half, low_ref, high_ref, packed_ref, start_ref, basis_ref, proj_ref, gram, held):
    windows = range(WIN_DEV)
    pitch = up(half, SUB)
    extra = half - LANES
    for k in range(BLOCKS):
        gram[k, :, :LANES] = packed_ref[pitch * k : pitch * k + half]
        gram[k, :, LANES:] = packed_ref[
            pitch * BLOCKS : pitch * BLOCKS + half, extra * k : extra * k + extra
        ]
    for w in windows:
        held[w, 0] = start_ref[:half]
        held[w, 1] = start_ref[half:]

    def step(_, carry):
        images = []
        for w in windows:
            top, cross, low = gram[2 * w], gram[2 * w + 1], gram[2 * w + 2]
            above, below = held[w, 0], held[w, 1]
            images.append(
                (
                    dot(top, above, 1, 0) + dot(cross, below, 1, 0),
                    dot(cross, above, 0, 0) + dot(low, below, 1, 0),
                )
            )
        inverses = inverse_factors([dot(a, a, 0, 0) + dot(b, b, 0, 0) for a, b in images])
        for w in windows:
            for h in range(2):
                held[w, h] = dot(images[w][h], inverses[w], 1, 1)
        return carry

    lax.fori_loop(0, ITERS, step, 0)
    columns = lax.broadcasted_iota(jnp.int32, (1, K), 1)
    for w in windows:
        keep = ((columns >= low_ref[w]) & (columns < high_ref[w])).astype(jnp.float32)
        basis_ref[w, :half] = held[w, 0]
        basis_ref[w, half:] = held[w, 1]
        for i in range(2):
            for j in range(2):
                proj_ref[w, i, j] = dot(held[w, i] * keep, held[w, j], 1, 1).astype(jnp.bfloat16)


def iterate(packed, start, low, high):
    half = start.shape[0] // 2
    return pl.pallas_call(
        functools.partial(iterate_kernel, half),
        out_shape=(
            jax.ShapeDtypeStruct((WIN_DEV, 2 * half, K), jnp.float32),
            jax.ShapeDtypeStruct((WIN_DEV, 2, 2, half, half), jnp.bfloat16),
        ),
        in_specs=[SMEM, SMEM, VMEM, VMEM],
        out_specs=(VMEM, VMEM),
        scratch_shapes=[
            pltpu.VMEM((BLOCKS, half, half), jnp.float32),
            pltpu.VMEM((WIN_DEV, 2, half, K), jnp.float32),
        ],
        cost_estimate=pl.CostEstimate(flops=40_000_000_000, bytes_accessed=1_000_000, transcendentals=0),
        name="iterate",
    )(low, high, packed, start)


def filter_kernel(half, place_ref, proj_ref, *refs):
    own, arrived, tail, power_ref = refs[:2], refs[2:4], refs[4:6], refs[6]
    front = place_ref[0] == 0
    for w in range(WIN_DEV):
        total = 0.0
        for part in range(2):
            above = own[part][w]
            if w == 0:
                below = own[part][1]
            else:
                below = jnp.where(front, arrived[part][...], tail[part][...])
            for i in range(2):
                rows = dot(proj_ref[w, i, 0], above, 1, 0, None)
                rows += dot(proj_ref[w, i, 1], below, 1, 0, None)
                total += jnp.sum(rows * rows, axis=0, keepdims=True)
        power_ref[w : w + 1] = total / (2 * half)


def filtered_power(place, projs, own, arrived, tail):
    _, half, columns = own.shape
    pixels = columns // 2
    tile = 512
    count = pixels // tile
    return pl.pallas_call(
        functools.partial(filter_kernel, half),
        out_shape=jax.ShapeDtypeStruct((WIN_DEV, pixels), jnp.float32),
        grid=(count,),
        in_specs=[
            SMEM,
            pl.BlockSpec(projs.shape, lambda i: (0, 0, 0, 0, 0)),
            pl.BlockSpec((2, half, tile), lambda i: (0, 0, i)),
            pl.BlockSpec((2, half, tile), lambda i: (0, 0, i + count)),
            pl.BlockSpec((half, tile), lambda i: (0, i)),
            pl.BlockSpec((half, tile), lambda i: (0, i)),
            pl.BlockSpec((half, tile), lambda i: (0, i)),
            pl.BlockSpec((half, tile), lambda i: (0, i + count)),
        ],
        out_specs=pl.BlockSpec((WIN_DEV, tile), lambda i: (0, i)),
        name="filter",
    )(place, projs, own, own, *arrived, tail, tail)


def body(iq, tail_frames, start_basis, low_rank, high_rank):
    assert lax.axis_size("tm") == 2
    half = iq.shape[0] // WIN_DEV
    place = lax.axis_index("tm")
    front = place == 0
    place = place.reshape(1).astype(jnp.int32)
    own = iq.reshape(WIN_DEV, half, -1)
    middle = own.shape[2] // 2
    swapped = lax.ppermute(
        jnp.where(front, own[1, :, middle:], own[0, :, :middle]), "tm", [(0, 1), (1, 0)]
    )
    tail = tail_frames.reshape(half, -1)
    rows = up(up(half, SUB) * (BLOCKS + 1), SUB * lax.axis_size("pix"))
    packed = gram_blocks(own, tail, rows)
    crossing = cross_block(place, own, swapped, packed)
    summed = sum_over_pix(packed, crossing, half)
    late, summed = lax.optimization_barrier((own[0, :, middle:], summed))
    late = lax.ppermute(late, "tm", [(1, 0)])
    bases, projs = iterate(summed, start_basis, low_rank, high_rank)
    return (filtered_power(place, projs, own, (swapped, late), tail), bases)


def solution(mesh):
    placed = (P("tm", None, "pix"), P(None, None, "pix"), P(), P("tm"), P("tm"))
    return jax.shard_map(
        body,
        mesh=mesh,
        in_specs=placed,
        out_specs=(P("tm", "pix"), P("tm", None, None)),
        check_vma=False,
    )
```
